32 devices in a mesh: cell: 8 (over y, x, core), narrow: 4 (over z).
Axes of the slice: x: 2, y: 2, z: 4, core: 2. Of those that a mesh axis runs over, the one named last changes fastest.
Arguments:
- snapshots: bfloat16 [4096, 4096], P('cell', 'narrow'), may hold values from -6 to 6
- cell_volume: float32 [4096], P('cell'), may hold values from 0.1 to 10
- mode_vectors: bfloat16 [4096, 512], P('narrow'), may hold values from -0.09375 to 0.09375
- mode_scale: float32 [512], replicated, may hold values from 0.25 to 4
- interp_weights: bfloat16 [4096, 4096], P('cell', 'narrow'), may hold values from -0.09375 to 0.09375
Outputs:
- gram_matrix: float32 [4096, 4096], P('cell', 'narrow')
- fields: bfloat16 [4096, 4096], P('cell', 'narrow')
The draws below stay inside these ranges and needn't reach their ends.
All inputs are finite; a program needn't handle non-finite values.
Results may differ from the reference program's by a relative error of at most 0.0064.
Values may be sent and summed in bfloat16 or wider, within the bound.
A program may use at most 128 MiB of HBM per device.

```python
import math
import jax
import jax.numpy as jnp
from jax import lax

MODES = 512
CELLS = 4096
NSNAP = 4096
NCOND = 4096


def strengthened(drawn, key, source, target, shards_of, factor):
    def block_of(dim):
        return (jnp.arange(drawn.shape[dim]) // (drawn.shape[dim] // shards_of)).reshape((-1,) + (1,) * (drawn.ndim - 1 - dim))

    first = jax.random.permutation(key, shards_of)[block_of(target)]
    second = (block_of(target) + shards_of // 2) % shards_of
    return jnp.where((block_of(source) == first) | (block_of(source) == second), factor * drawn, drawn)


def block_levels(own_key, dims, split, low, top_value):
    factor_of = 1.0
    for position, blocks in split:
        steps = jax.random.uniform(jax.random.fold_in(jax.random.fold_in(own_key, 6), position), (blocks,), jnp.float32, low / len(split), top_value / len(split))
        factor_of = factor_of * jnp.repeat(jnp.exp(steps), dims[position] // blocks).reshape((-1,) + (1,) * (len(dims) - 1 - position))
    return factor_of


def gaussian(stream_key, shape, scale, most, split=(), dtype=jnp.bfloat16):
    factor_of = block_levels(stream_key, shape, split, -0.22, 0.18) if split else 1.0
    entries = jax.random.normal(stream_key, shape, jnp.float32) * scale * factor_of
    return jnp.minimum(jnp.maximum(entries, -most), most).astype(dtype)


def heavy_noise(rng, extent, spread, most, split, heavy, kind=jnp.bfloat16):
    entries = spread * jax.random.normal(rng, extent, jnp.float32)
    if split:
        entries = entries * block_levels(rng, extent, split, -0.22, 0.18)
    return jnp.clip(strengthened(entries, jax.random.fold_in(rng, 3), *heavy), -most, most).astype(kind)


def setup_inputs(seed: int = 0) -> dict:
    streams_of = jax.random.split(jax.random.key(seed), 6)
    return {
        "snapshots": heavy_noise(streams_of[0], (CELLS, NSNAP), 1.0, 6.0, ((0, 8), (1, 4)), (0, 1, 8, 2.0)),
        "cell_volume": jnp.clip(jnp.exp(math.log(10.0) - 4.6051702 * jax.random.uniform(streams_of[1], (CELLS,), jnp.float32) ** block_levels(streams_of[1], (CELLS,), ((0, 8),), -0.2, 0.2)), 0.1, 10.0),
        "mode_vectors": gaussian(streams_of[2], (NSNAP, MODES), NSNAP ** -0.5, 0.09375, ((0, 4),)),
        "mode_scale": jnp.clip(jnp.exp(jax.random.uniform(streams_of[3], (MODES,), jnp.float32, math.log(0.25), math.log(4.0))), 0.25, 4.0),
        "interp_weights": gaussian(streams_of[4], (NSNAP, NCOND), NSNAP ** -0.5, 0.09375, ((0, 8), (1, 4))),
    }


def reference(snapshots, cell_volume, mode_vectors, mode_scale, interp_weights):
    weighted = (snapshots.astype(jnp.float32) * cell_volume[:, None]).astype(jnp.bfloat16)
    gram_matrix = lax.dot_general(snapshots, weighted, (((0,), (0,)), ((), ())), preferred_element_type=jnp.float32) / CELLS
    summed = lax.dot_general(mode_vectors.astype(jnp.float32), gram_matrix, (((0,), (1,)), ((), ())), precision=lax.Precision.HIGHEST)
    coefficients = (mode_scale[:, None] * summed).astype(jnp.bfloat16)
    new_coeffs = jnp.dot(coefficients, interp_weights, preferred_element_type=jnp.float32).astype(jnp.bfloat16)
    mode_shapes = jnp.dot(snapshots, mode_vectors, preferred_element_type=jnp.float32).astype(jnp.bfloat16)
    fields = jnp.dot(mode_shapes, new_coeffs, preferred_element_type=jnp.float32).astype(jnp.bfloat16)
    return gram_matrix, fields
```

```python
import jax
import jax.numpy as jnp
from jax import lax
from jax.sharding import PartitionSpec as P


def shards(snapshots, cell_volume, mode_vectors, mode_scale, interp_weights):
    f32, bf16 = jnp.float32, jnp.bfloat16
    n_cell, n_narrow = lax.axis_size("cell"), lax.axis_size("narrow")
    total_cells = snapshots.shape[0] * n_cell
    rows = interp_weights.shape[0]
    weighted = (snapshots.astype(f32) * cell_volume[:, None]).astype(bf16)

    partial_shapes = jnp.dot(snapshots, mode_vectors, preferred_element_type=f32)
    mode_shapes = lax.psum(partial_shapes, "narrow").astype(bf16)

    gathered = lax.all_gather(snapshots, "narrow", axis=1, tiled=True)
    scaled_shapes = (
        mode_shapes.astype(f32) * (cell_volume / total_cells)[:, None] * mode_scale[None, :]
    ).astype(bf16)
    partial_coeffs = lax.dot_general(
        gathered, scaled_shapes, (((0,), (0,)), ((), ())), preferred_element_type=f32
    ).astype(bf16)
    coeffs = lax.psum_scatter(partial_coeffs, "cell", scatter_dimension=0, tiled=True)
    partial_new = lax.dot_general(
        coeffs, interp_weights, (((0,), (0,)), ((), ())), preferred_element_type=f32
    )
    new_coeffs = lax.psum(partial_new, "cell").astype(bf16)
    fields = jnp.dot(mode_shapes, new_coeffs, preferred_element_type=f32).astype(bf16)

    partial_gram = (
        lax.dot_general(gathered, weighted, (((0,), (0,)), ((), ())), preferred_element_type=f32)
        / total_cells
    ).astype(bf16)
    gram = lax.psum_scatter(partial_gram, "cell", scatter_dimension=0, tiled=True)
    return (gram.astype(f32), fields)


def solution(mesh):
    return jax.shard_map(
        shards,
        mesh=mesh,
        in_specs=(P("cell", "narrow"), P("cell"), P("narrow", None), P(), P("cell", "narrow")),
        out_specs=(P("cell", "narrow"), P("cell", "narrow")),
        check_vma=False,
    )
```

```python
import functools

import jax
import jax.numpy as jnp
from jax import lax
from jax.experimental import pallas as pl
from jax.experimental.pallas import tpu as pltpu
from jax.sharding import PartitionSpec as P

F32, BF16 = jnp.float32, jnp.bfloat16
MESH = pl.DeviceIdType.MESH
CHUNKS = 4


def shards_xla(snapshots, cell_volume, mode_vectors, mode_scale, interp_weights):
    f32, bf16 = jnp.float32, jnp.bfloat16
    n_cell, n_narrow = lax.axis_size("cell"), lax.axis_size("narrow")
    total_cells = snapshots.shape[0] * n_cell
    rows = interp_weights.shape[0]
    weighted = (snapshots.astype(f32) * cell_volume[:, None]).astype(bf16)

    partial_shapes = jnp.dot(snapshots, mode_vectors, preferred_element_type=f32)
    mode_shapes = lax.psum(partial_shapes, "narrow").astype(bf16)

    gathered = lax.all_gather(snapshots, "narrow", axis=1, tiled=True)
    scaled_shapes = (
        mode_shapes.astype(f32) * (cell_volume / total_cells)[:, None] * mode_scale[None, :]
    ).astype(bf16)
    partial_coeffs = lax.dot_general(
        gathered, scaled_shapes, (((0,), (0,)), ((), ())), preferred_element_type=f32
    ).astype(bf16)
    coeffs = lax.psum_scatter(partial_coeffs, "cell", scatter_dimension=0, tiled=True)
    partial_new = lax.dot_general(
        coeffs, interp_weights, (((0,), (0,)), ((), ())), preferred_element_type=f32
    )
    new_coeffs = lax.psum(partial_new, "cell").astype(bf16)
    fields = jnp.dot(mode_shapes, new_coeffs, preferred_element_type=f32).astype(bf16)

    partial_gram = (
        lax.dot_general(gathered, weighted, (((0,), (0,)), ((), ())), preferred_element_type=f32)
        / total_cells
    ).astype(bf16)
    gram = lax.psum_scatter(partial_gram, "cell", scatter_dimension=0, tiled=True)
    return (gram.astype(f32), fields)


def kernel(
    C, Z, total, s, volb, v, scale, w, gram, fields,
    sg, sp, volp, wf, gsend, grecv, mpart, mrecv, mg, mgp, dm, csend, crecv, cb, ksend, krecv, kg,
    loc_sem, ps_sem, pr_sem, xs_sem, xr_sem, zs_sem, zr_sem, gs_sem, gr_sem,
    ms_sem, mr_sem, as_sem, ar_sem, cs_sem, cr_sem, bs_sem, br_sem,
    ks_sem, kr_sem, ls_sem, lr_sem,
):
    c, z = lax.axis_index("cell"), lax.axis_index("narrow")
    groups = C // 2
    p, k = lax.div(c, 2), lax.rem(c, 2)
    mate = 2 * p + 1 - k
    rows, cols = s.shape
    modes = v.shape[1]
    half = cols // 2
    cw = half // CHUNKS
    mrows = rows // Z
    krows = modes // C

    def remote(src, dst, ssem, rsem, cell, narrow):
        return pltpu.make_async_remote_copy(
            src_ref=src, dst_ref=dst, send_sem=ssem, recv_sem=rsem,
            device_id={"cell": cell, "narrow": narrow}, device_id_type=MESH,
        )

    def other(me, step, n):
        return lax.rem(me + step, n)

    barrier = pltpu.get_barrier_semaphore()
    for d in range(1, C):
        pl.semaphore_signal(
            barrier, inc=1, device_id={"cell": other(c, d, C), "narrow": z}, device_id_type=MESH
        )
    for d in range(1, Z):
        pl.semaphore_signal(
            barrier, inc=1, device_id={"cell": c, "narrow": other(z, d, Z)}, device_id_type=MESH
        )
    pl.semaphore_wait(barrier, C + Z - 2)

    mine = pl.ds(pl.multiple_of(k * rows, rows), rows)
    theirs = pl.ds(pl.multiple_of((1 - k) * rows, rows), rows)

    def local_copy(h):
        lanes = pl.ds(pl.multiple_of(k * half + h * cw, cw), cw)
        return pltpu.make_async_copy(s.at[:, lanes], sg.at[z, h, mine], loc_sem.at[h])

    def mate_copy(h):
        lanes = pl.ds(pl.multiple_of((1 - k) * half + h * cw, cw), cw)
        return remote(
            s.at[:, lanes], sg.at[z, h, mine], ps_sem.at[h], pr_sem.at[h], mate, z
        )

    block_copy = remote(s, sp, xs_sem.at[0], xr_sem.at[0], mate, z)
    vol_copy = remote(volb, volp, xs_sem.at[1], xr_sem.at[1], mate, z)
    for h in range(CHUNKS):
        local_copy(h).start()
        mate_copy(h).start()
    vol_copy.start()
    block_copy.start()

    mpart[...] = jnp.dot(s[...], v[...], preferred_element_type=F32)

    def shape_rows(b):
        return pl.ds(pl.multiple_of(b * mrows, mrows), mrows)

    def shape_send(d):
        t = other(z, d, Z)
        return remote(mpart.at[shape_rows(t)], mrecv.at[z], ms_sem.at[t], mr_sem.at[z], c, t)

    for d in range(1, Z):
        shape_send(d).start()

    def chain(side, b, h):
        to = jnp.minimum(z + 1, Z - 1) if side == 0 else jnp.maximum(z - 1, 0)
        return remote(sg.at[b, h], sg.at[b, h], zs_sem.at[side, b, h], zr_sem.at[b, h], c, to)

    for h in range(CHUNKS):
        local_copy(h).wait()
        mate_copy(h).wait_recv()

        @pl.when(z < Z - 1)
        def _():
            chain(0, z, h).start()

        @pl.when(z > 0)
        def _():
            chain(1, z, h).start()

    wf[mine, :] = (s[...].astype(F32) * volb[:, :1]).astype(BF16)
    vol_copy.wait_recv()
    block_copy.wait_recv()
    wf[theirs, :] = (sp[...].astype(F32) * volp[:, :1]).astype(BF16)

    def gram_send(b, h):
        return remote(
            gsend.at[b, h], grecv.at[p, h], gs_sem.at[b, h], gr_sem.at[p, h], 2 * b + k, z
        )

    def gram_term(b, h):
        term = lax.dot_general(
            sg[b, h], wf[...], (((0,), (0,)), ((), ())), preferred_element_type=F32
        ) * (1.0 / total)

        @pl.when(b == p)
        def _():
            gram[pl.ds(pl.multiple_of(h * cw, cw), cw), :] = term

        @pl.when(b != p)
        def _():
            gsend[b, h] = term.astype(BF16)
            gram_send(b, h).start()

    @pl.loop(0, CHUNKS)
    def _(h):
        gram_term(z, h)

    acc = mpart[shape_rows(z), :]
    for d in range(1, Z):
        q = other(z, d, Z)
        remote(mpart.at[shape_rows(z)], mrecv.at[q], ms_sem.at[q], mr_sem.at[q], c, q).wait_recv()
        acc = acc + mrecv[q]
    mg[shape_rows(z), :] = acc.astype(BF16)

    def shape_share(d, b):
        t = other(z, d, Z)
        return remote(mg.at[shape_rows(b)], mg.at[shape_rows(b)], as_sem.at[t], ar_sem.at[b], c, t)

    for d in range(1, Z):
        shape_share(d, z).start()

    def hop(t, h):
        for side in (0, 1):
            b = z - t if side == 0 else z + t
            there = b >= 0 if side == 0 else b < Z
            onward = z < Z - 1 if side == 0 else z > 0

            @pl.when(there)
            def _():
                chain(side, b, h).wait_recv()

                @pl.when(onward)
                def _():
                    chain(side, b, h).start()

                gram_term(b, h)

    def hops(t):
        @pl.loop(0, CHUNKS)
        def _(h):
            hop(t, h)

    hops(1)

    for d in range(1, Z):
        shape_share(d, other(z, d, Z)).wait_recv()
        shape_send(d).wait_send()
    mate_shapes = remote(mg, mgp, xs_sem.at[2], xr_sem.at[2], mate, z)
    mate_shapes.start()
    dm[mine, :] = (mg[...].astype(F32) * volb[:, :1]).astype(BF16)
    mate_shapes.wait_recv()
    dm[theirs, :] = (mgp[...].astype(F32) * volp[:, :1]).astype(BF16)
    diagonal = p == z

    def coeff_send():
        return remote(csend, crecv.at[p], cs_sem.at[0], cr_sem.at[p], 2 * z + k, z)

    def coeff_share(side):
        to = jnp.minimum(z + 1, Z - 1) if side == 0 else jnp.maximum(z - 1, 0)
        return remote(cb, cb, bs_sem.at[side], br_sem.at[0], c, to)

    @pl.loop(0, CHUNKS)
    def _(h):
        at = pl.ds(pl.multiple_of(h * cw, cw), cw)
        term = lax.dot_general(
            sg[z, h], dm[...], (((0,), (0,)), ((), ())), preferred_element_type=F32
        )

        @pl.when(diagonal)
        def _():
            mpart[at, :] = term

        @pl.when(p != z)
        def _():
            csend[at, :] = term.astype(BF16)

    @pl.when(p != z)
    def _():
        coeff_send().start()

    if Z > 2:
        hops(2)

    @pl.when(diagonal)
    def _():
        total_c = mpart[...]
        for d in range(1, groups):
            q = other(p, d, groups)
            remote(
                csend, crecv.at[q], cs_sem.at[0], cr_sem.at[q], 2 * q + k, z
            ).wait_recv()
            total_c = total_c + crecv[q].astype(F32)
        cb[...] = (total_c * (scale[...] * (1.0 / total))).astype(BF16)

        @pl.when(z < Z - 1)
        def _():
            coeff_share(0).start()

        @pl.when(z > 0)
        def _():
            coeff_share(1).start()

    @pl.when(z > p)
    def _():
        coeff_share(0).wait_recv()

        @pl.when(z < Z - 1)
        def _():
            coeff_share(0).start()

    @pl.when(z < p)
    def _():
        coeff_share(1).wait_recv()

        @pl.when(z > 0)
        def _():
            coeff_share(1).start()

    def new_send(t):
        return remote(ksend.at[t], krecv.at[c], ks_sem.at[t], kr_sem.at[c], t, z)

    part = lax.dot_general(cb[...], w[...], (((0,), (0,)), ((), ())), preferred_element_type=F32)
    ksend[...] = part.reshape(C, krows, w.shape[1]).astype(BF16)
    for d in range(1, C):
        new_send(other(c, d, C)).start()

    for t in range(3, Z):
        hops(t)

    new = ksend[c].astype(F32)
    for d in range(1, C):
        q = other(c, d, C)
        remote(ksend.at[q], krecv.at[q], ks_sem.at[q], kr_sem.at[q], q, z).wait_recv()
        new = new + krecv[q].astype(F32)
    kg[c] = new.astype(BF16)

    def new_share(t, b):
        return remote(kg.at[b], kg.at[b], ls_sem.at[t], lr_sem.at[b], t, z)

    for d in range(1, C):
        new_share(other(c, d, C), c).start()

    @pl.loop(0, CHUNKS)
    def _(h):
        at = pl.ds(pl.multiple_of(h * cw, cw), cw)
        acc = gram[at, :]
        for d in range(1, groups):
            q = other(p, d, groups)
            remote(
                gsend.at[q, h], grecv.at[q, h], gs_sem.at[q, h], gr_sem.at[q, h], 2 * q + k, z
            ).wait_recv()
            acc = acc + grecv[q, h].astype(F32)
        gram[at, :] = acc

    for d in range(1, C):
        q = other(c, d, C)
        new_share(q, q).wait_recv()
    fields[...] = jnp.dot(
        mg[...], kg[...].reshape(modes, w.shape[1]), preferred_element_type=F32
    ).astype(BF16)

    vol_copy.wait_send()
    block_copy.wait_send()
    mate_shapes.wait_send()
    for h in range(CHUNKS):
        mate_copy(h).wait_send()
    for d in range(1, Z):
        shape_share(d, z).wait_send()
    for d in range(1, C):
        new_send(other(c, d, C)).wait_send()
        new_share(other(c, d, C), c).wait_send()

    @pl.when(p != z)
    def _():
        coeff_send().wait_send()

    @pl.when((z >= p) & (z < Z - 1))
    def _():
        coeff_share(0).wait_send()

    @pl.when((z <= p) & (z > 0))
    def _():
        coeff_share(1).wait_send()

    @pl.loop(0, CHUNKS)
    def _(h):
        for b in range(Z):
            @pl.when((b <= z) & (z < Z - 1))
            def _():
                chain(0, b, h).wait_send()

            @pl.when((b >= z) & (z > 0))
            def _():
                chain(1, b, h).wait_send()

        for d in range(1, groups):
            gram_send(other(p, d, groups), h).wait_send()


def shards_kernel(snapshots, cell_volume, mode_vectors, mode_scale, interp_weights):
    C, Z = lax.axis_size("cell"), lax.axis_size("narrow")
    groups = C // 2
    rows, cols = snapshots.shape
    modes = mode_vectors.shape[1]
    conds = interp_weights.shape[1]
    half = cols // 2
    cw = half // CHUNKS
    dma = pltpu.SemaphoreType.DMA
    volb = jnp.broadcast_to(cell_volume[:, None], (rows, 128))
    vmem = pl.BlockSpec(memory_space=pltpu.VMEM)
    return pl.pallas_call(
        functools.partial(kernel, C, Z, rows * C),
        out_shape=(
            jax.ShapeDtypeStruct((half, cols), F32),
            jax.ShapeDtypeStruct((rows, conds), BF16),
        ),
        in_specs=[vmem] * 5,
        out_specs=(vmem, vmem),
        scratch_shapes=[
            pltpu.VMEM((Z, CHUNKS, 2 * rows, cw), BF16),
            pltpu.VMEM((rows, cols), BF16),
            pltpu.VMEM((rows, 128), F32),
            pltpu.VMEM((2 * rows, cols), BF16),
            pltpu.VMEM((groups, CHUNKS, cw, cols), BF16),
            pltpu.VMEM((groups, CHUNKS, cw, cols), BF16),
            pltpu.VMEM((rows, modes), F32),
            pltpu.VMEM((Z, rows // Z, modes), F32),
            pltpu.VMEM((rows, modes), BF16),
            pltpu.VMEM((rows, modes), BF16),
            pltpu.VMEM((2 * rows, modes), BF16),
            pltpu.VMEM((half, modes), BF16),
            pltpu.VMEM((groups, half, modes), BF16),
            pltpu.VMEM((half, modes), BF16),
            pltpu.VMEM((C, modes // C, conds), BF16),
            pltpu.VMEM((C, modes // C, conds), BF16),
            pltpu.VMEM((C, modes // C, conds), BF16),
            dma((CHUNKS,)), dma((CHUNKS,)), dma((CHUNKS,)),
            dma((3,)), dma((3,)),
            dma((2, Z, CHUNKS)), dma((Z, CHUNKS)),
            dma((groups, CHUNKS)), dma((groups, CHUNKS)),
            dma((Z,)), dma((Z,)), dma((Z,)), dma((Z,)),
            dma((1,)), dma((groups,)),
            dma((2,)), dma((1,)),
            dma((C,)), dma((C,)), dma((C,)), dma((C,)),
        ],
        compiler_params=pltpu.CompilerParams(
            collective_id=0, has_side_effects=True, vmem_limit_bytes=52 * 1024 * 1024
        ),
    )(snapshots, volb, mode_vectors, mode_scale[None, :], interp_weights)


def shards(snapshots, cell_volume, mode_vectors, mode_scale, interp_weights):
    C, Z = lax.axis_size("cell"), lax.axis_size("narrow")
    rows, cols = snapshots.shape
    modes = mode_vectors.shape[1]
    fits = (
        C == 2 * Z
        and cols % (2 * 128 * CHUNKS) == 0
        and rows % (16 * Z) == 0
        and modes % (16 * C) == 0
        and interp_weights.shape[0] == rows == cols // 2
        and rows * cols <= 512 * 1024
        and interp_weights.shape[1] <= 1024
        and modes <= 512
    )
    run = shards_kernel if fits else shards_xla
    return run(snapshots, cell_volume, mode_vectors, mode_scale, interp_weights)


def solution(mesh):
    return jax.shard_map(
        shards,
        mesh=mesh,
        in_specs=(P("cell", "narrow"), P("cell"), P("narrow", None), P(), P("cell", "narrow")),
        out_specs=(P("cell", "narrow"), P("cell", "narrow")),
        check_vma=False,
    )
```

```python
import functools

import jax
import jax.numpy as jnp
from jax import lax
from jax.experimental import pallas as pl
from jax.experimental.pallas import tpu as pltpu
from jax.sharding import PartitionSpec as P

F32, BF16 = jnp.float32, jnp.bfloat16
MESH = pl.DeviceIdType.MESH
CHUNKS = 4
LAG = 2


def shards_xla(snapshots, cell_volume, mode_vectors, mode_scale, interp_weights):
    f32, bf16 = jnp.float32, jnp.bfloat16
    n_cell, n_narrow = lax.axis_size("cell"), lax.axis_size("narrow")
    total_cells = snapshots.shape[0] * n_cell
    rows = interp_weights.shape[0]
    weighted = (snapshots.astype(f32) * cell_volume[:, None]).astype(bf16)

    partial_shapes = jnp.dot(snapshots, mode_vectors, preferred_element_type=f32)
    mode_shapes = lax.psum(partial_shapes, "narrow").astype(bf16)

    gathered = lax.all_gather(snapshots, "narrow", axis=1, tiled=True)
    scaled_shapes = (
        mode_shapes.astype(f32) * (cell_volume / total_cells)[:, None] * mode_scale[None, :]
    ).astype(bf16)
    partial_coeffs = lax.dot_general(
        gathered, scaled_shapes, (((0,), (0,)), ((), ())), preferred_element_type=f32
    ).astype(bf16)
    coeffs = lax.psum_scatter(partial_coeffs, "cell", scatter_dimension=0, tiled=True)
    partial_new = lax.dot_general(
        coeffs, interp_weights, (((0,), (0,)), ((), ())), preferred_element_type=f32
    )
    new_coeffs = lax.psum(partial_new, "cell").astype(bf16)
    fields = jnp.dot(mode_shapes, new_coeffs, preferred_element_type=f32).astype(bf16)

    partial_gram = (
        lax.dot_general(gathered, weighted, (((0,), (0,)), ((), ())), preferred_element_type=f32)
        / total_cells
    ).astype(bf16)
    gram = lax.psum_scatter(partial_gram, "cell", scatter_dimension=0, tiled=True)
    return (gram.astype(f32), fields)


def kernel(
    C, Z, total, s, volb, v, scale, w, gram, fields,
    sg, sp, volp, wf, gsend, grecv, rrecv, mpart, mrecv, mg, mgp, dm, csend, crecv, cb, ksend, krecv, kg,
    loc_sem, ps_sem, pr_sem, xs_sem, xr_sem, zs_sem, zr_sem, gs_sem, gr_sem, fs_sem, fr_sem,
    ms_sem, mr_sem, as_sem, ar_sem, cs_sem, cr_sem, bs_sem, br_sem,
    ks_sem, kr_sem, ls_sem, lr_sem,
):
    c, z = lax.axis_index("cell"), lax.axis_index("narrow")
    groups = C // 2
    p, k = lax.div(c, 2), lax.rem(c, 2)
    mate = 2 * p + 1 - k
    rows, cols = s.shape
    modes = v.shape[1]
    half = cols // 2
    cw = half // CHUNKS
    mrows = rows // Z
    krows = modes // C

    def remote(src, dst, ssem, rsem, cell, narrow):
        return pltpu.make_async_remote_copy(
            src_ref=src, dst_ref=dst, send_sem=ssem, recv_sem=rsem,
            device_id={"cell": cell, "narrow": narrow}, device_id_type=MESH,
        )

    def other(me, step, n):
        return lax.rem(me + step, n)

    barrier = pltpu.get_barrier_semaphore()
    for d in range(1, C):
        pl.semaphore_signal(
            barrier, inc=1, device_id={"cell": other(c, d, C), "narrow": z}, device_id_type=MESH
        )
    for d in range(1, Z):
        pl.semaphore_signal(
            barrier, inc=1, device_id={"cell": c, "narrow": other(z, d, Z)}, device_id_type=MESH
        )
    pl.semaphore_wait(barrier, C + Z - 2)

    mine = pl.ds(pl.multiple_of(k * rows, rows), rows)
    theirs = pl.ds(pl.multiple_of((1 - k) * rows, rows), rows)

    def local_copy(h):
        lanes = pl.ds(pl.multiple_of(k * half + h * cw, cw), cw)
        return pltpu.make_async_copy(s.at[:, lanes], sg.at[z, h, mine], loc_sem.at[h])

    def mate_copy(h):
        lanes = pl.ds(pl.multiple_of((1 - k) * half + h * cw, cw), cw)
        return remote(
            s.at[:, lanes], sg.at[z, h, mine], ps_sem.at[h], pr_sem.at[h], mate, z
        )

    block_copy = remote(s, sp, xs_sem.at[0], xr_sem.at[0], mate, z)
    vol_copy = remote(volb, volp, xs_sem.at[1], xr_sem.at[1], mate, z)
    for h in range(CHUNKS):
        local_copy(h).start()
        mate_copy(h).start()
    vol_copy.start()
    block_copy.start()

    mpart[...] = jnp.dot(s[...], v[...], preferred_element_type=F32)

    def shape_rows(b):
        return pl.ds(pl.multiple_of(b * mrows, mrows), mrows)

    def shape_send(d):
        t = other(z, d, Z)
        return remote(mpart.at[shape_rows(t)], mrecv.at[z], ms_sem.at[t], mr_sem.at[z], c, t)

    for d in range(1, Z):
        shape_send(d).start()

    def chain(side, b, h):
        to = jnp.minimum(z + 1, Z - 1) if side == 0 else jnp.maximum(z - 1, 0)
        return remote(sg.at[b, h], sg.at[b, h], zs_sem.at[side, b, h], zr_sem.at[b, h], c, to)

    for h in range(CHUNKS):
        local_copy(h).wait()
        mate_copy(h).wait_recv()

        @pl.when(z < Z - 1)
        def _():
            chain(0, z, h).start()

        @pl.when(z > 0)
        def _():
            chain(1, z, h).start()

    wf[mine, :] = (s[...].astype(F32) * volb[:, :1]).astype(BF16)
    vol_copy.wait_recv()
    block_copy.wait_recv()
    wf[theirs, :] = (sp[...].astype(F32) * volp[:, :1]).astype(BF16)

    def gram_send(b, h):
        return remote(
            gsend.at[b, h], grecv.at[p, h], gs_sem.at[b, h], gr_sem.at[p, h], 2 * b + k, z
        )

    def apart(b):
        return jnp.where(p // 2 == b // 2, 0, 2) + jnp.where(p % 2 == b % 2, 0, 1)

    def flip(b, d):
        row = 1 - b // 2 if d == 2 else b // 2
        col = 1 - b % 2 if d == 1 else b % 2
        return 2 * row + col

    def relays(b, h):
        odd = h % 2 == 1
        return (odd & (apart(b) == 1)) | ((h % 2 == 0) & (apart(b) == 2))

    def passes(b, h):
        return (b != p) & ((((h % 2) == 0) & (apart(b) == 1)) | (((h % 2) == 1) & (apart(b) == 2)))

    def across_send(b, h):
        to = jnp.where(h % 2 == 1, flip(b, 1), flip(b, 2))
        return remote(
            gsend.at[b, h], rrecv.at[b, h], fs_sem.at[b, h], fr_sem.at[b, h], 2 * to + k, z
        )

    def across_wait(b, h):
        return remote(
            gsend.at[b, h], rrecv.at[b, h], fs_sem.at[b, h], fr_sem.at[b, h],
            2 * other(p, 1, groups) + k, z,
        )

    def gram_term(b, h):
        term = lax.dot_general(
            sg[b, h], wf[...], (((0,), (0,)), ((), ())), preferred_element_type=F32
        ) * (1.0 / total)

        @pl.when(b == p)
        def _():
            gram[pl.ds(pl.multiple_of(h * cw, cw), cw), :] = term

        @pl.when(b != p)
        def _():
            gsend[b, h] = term.astype(BF16)

        @pl.when(apart(b) == 3)
        def _():
            across_send(b, h).start()

        @pl.when(passes(b, h))
        def _():
            gram_send(b, h).start()

    def relay(b, h):
        @pl.when(relays(b, h))
        def _():
            across_wait(b, h).wait_recv()
            gsend[b, h] = (gsend[b, h].astype(F32) + rrecv[b, h].astype(F32)).astype(BF16)
            gram_send(b, h).start()

    def relay_event(e):
        @pl.when(e >= 0)
        def _():
            t, h = e // CHUNKS, e % CHUNKS
            for side in (0, 1):
                b = z - t if side == 0 else z + t
                there = (b >= 0) if side == 0 else (b < Z) & (t > 0)

                @pl.when(there)
                def _():
                    relay(b, h)

    @pl.loop(0, CHUNKS)
    def _(h):
        gram_term(z, h)
        relay_event(h - LAG)

    acc = mpart[shape_rows(z), :]
    for d in range(1, Z):
        q = other(z, d, Z)
        remote(mpart.at[shape_rows(z)], mrecv.at[q], ms_sem.at[q], mr_sem.at[q], c, q).wait_recv()
        acc = acc + mrecv[q]
    mg[shape_rows(z), :] = acc.astype(BF16)

    def shape_share(d, b):
        t = other(z, d, Z)
        return remote(mg.at[shape_rows(b)], mg.at[shape_rows(b)], as_sem.at[t], ar_sem.at[b], c, t)

    for d in range(1, Z):
        shape_share(d, z).start()

    def hop(t, h):
        for side in (0, 1):
            b = z - t if side == 0 else z + t
            there = b >= 0 if side == 0 else b < Z
            onward = z < Z - 1 if side == 0 else z > 0

            @pl.when(there)
            def _():
                chain(side, b, h).wait_recv()

                @pl.when(onward)
                def _():
                    chain(side, b, h).start()

                gram_term(b, h)

    def hops(t):
        @pl.loop(0, CHUNKS)
        def _(h):
            hop(t, h)
            relay_event(t * CHUNKS + h - LAG)

    hops(1)

    for d in range(1, Z):
        shape_share(d, other(z, d, Z)).wait_recv()
        shape_send(d).wait_send()
    mate_shapes = remote(mg, mgp, xs_sem.at[2], xr_sem.at[2], mate, z)
    mate_shapes.start()
    dm[mine, :] = (mg[...].astype(F32) * volb[:, :1]).astype(BF16)
    mate_shapes.wait_recv()
    dm[theirs, :] = (mgp[...].astype(F32) * volp[:, :1]).astype(BF16)
    diagonal = p == z

    def coeff_send():
        return remote(csend, crecv.at[p], cs_sem.at[0], cr_sem.at[p], 2 * z + k, z)

    def coeff_share(side):
        to = jnp.minimum(z + 1, Z - 1) if side == 0 else jnp.maximum(z - 1, 0)
        return remote(cb, cb, bs_sem.at[side], br_sem.at[0], c, to)

    @pl.loop(0, CHUNKS)
    def _(h):
        at = pl.ds(pl.multiple_of(h * cw, cw), cw)
        term = lax.dot_general(
            sg[z, h], dm[...], (((0,), (0,)), ((), ())), preferred_element_type=F32
        )

        @pl.when(diagonal)
        def _():
            mpart[at, :] = term

        @pl.when(p != z)
        def _():
            csend[at, :] = term.astype(BF16)

    @pl.when(p != z)
    def _():
        coeff_send().start()

    if Z > 2:
        hops(2)

    @pl.when(diagonal)
    def _():
        total_c = mpart[...]
        for d in range(1, groups):
            q = other(p, d, groups)
            remote(
                csend, crecv.at[q], cs_sem.at[0], cr_sem.at[q], 2 * q + k, z
            ).wait_recv()
            total_c = total_c + crecv[q].astype(F32)
        cb[...] = (total_c * (scale[...] * (1.0 / total))).astype(BF16)

        @pl.when(z < Z - 1)
        def _():
            coeff_share(0).start()

        @pl.when(z > 0)
        def _():
            coeff_share(1).start()

    @pl.when(z > p)
    def _():
        coeff_share(0).wait_recv()

        @pl.when(z < Z - 1)
        def _():
            coeff_share(0).start()

    @pl.when(z < p)
    def _():
        coeff_share(1).wait_recv()

        @pl.when(z > 0)
        def _():
            coeff_share(1).start()

    def new_send(t):
        return remote(ksend.at[t], krecv.at[c], ks_sem.at[t], kr_sem.at[c], t, z)

    part = lax.dot_general(cb[...], w[...], (((0,), (0,)), ((), ())), preferred_element_type=F32)
    ksend[...] = part.reshape(C, krows, w.shape[1]).astype(BF16)
    for d in range(1, C):
        new_send(other(c, d, C)).start()

    for t in range(3, Z):
        hops(t)

    for e in range(Z * CHUNKS - LAG, Z * CHUNKS):
        relay_event(jnp.int32(e))

    new = ksend[c].astype(F32)
    for d in range(1, C):
        q = other(c, d, C)
        remote(ksend.at[q], krecv.at[q], ks_sem.at[q], kr_sem.at[q], q, z).wait_recv()
        new = new + krecv[q].astype(F32)
    kg[c] = new.astype(BF16)

    def new_share(t, b):
        return remote(kg.at[b], kg.at[b], ls_sem.at[t], lr_sem.at[b], t, z)

    for d in range(1, C):
        new_share(other(c, d, C), c).start()

    @pl.loop(0, CHUNKS)
    def _(h):
        at = pl.ds(pl.multiple_of(h * cw, cw), cw)
        acc = gram[at, :]
        for d in (1, 2):
            q = flip(p, d)
            remote(
                gsend.at[q, h], grecv.at[q, h], gs_sem.at[q, h], gr_sem.at[q, h], 2 * q + k, z
            ).wait_recv()
            acc = acc + grecv[q, h].astype(F32)
        gram[at, :] = acc

    for d in range(1, C):
        q = other(c, d, C)
        new_share(q, q).wait_recv()
    fields[...] = jnp.dot(
        mg[...], kg[...].reshape(modes, w.shape[1]), preferred_element_type=F32
    ).astype(BF16)

    vol_copy.wait_send()
    block_copy.wait_send()
    mate_shapes.wait_send()
    for h in range(CHUNKS):
        mate_copy(h).wait_send()
    for d in range(1, Z):
        shape_share(d, z).wait_send()
    for d in range(1, C):
        new_send(other(c, d, C)).wait_send()
        new_share(other(c, d, C), c).wait_send()

    @pl.when(p != z)
    def _():
        coeff_send().wait_send()

    @pl.when((z >= p) & (z < Z - 1))
    def _():
        coeff_share(0).wait_send()

    @pl.when((z <= p) & (z > 0))
    def _():
        coeff_share(1).wait_send()

    @pl.loop(0, CHUNKS)
    def _(h):
        for b in range(Z):
            @pl.when((b <= z) & (z < Z - 1))
            def _():
                chain(0, b, h).wait_send()

            @pl.when((b >= z) & (z > 0))
            def _():
                chain(1, b, h).wait_send()

        for d in (1, 2):
            gram_send(flip(p, d), h).wait_send()
        across_send(flip(flip(p, 1), 2), h).wait_send()


def shards_kernel(snapshots, cell_volume, mode_vectors, mode_scale, interp_weights):
    C, Z = lax.axis_size("cell"), lax.axis_size("narrow")
    groups = C // 2
    rows, cols = snapshots.shape
    modes = mode_vectors.shape[1]
    conds = interp_weights.shape[1]
    half = cols // 2
    cw = half // CHUNKS
    dma = pltpu.SemaphoreType.DMA
    volb = jnp.broadcast_to(cell_volume[:, None], (rows, 128))
    vmem = pl.BlockSpec(memory_space=pltpu.VMEM)
    return pl.pallas_call(
        functools.partial(kernel, C, Z, rows * C),
        out_shape=(
            jax.ShapeDtypeStruct((half, cols), F32),
            jax.ShapeDtypeStruct((rows, conds), BF16),
        ),
        in_specs=[vmem] * 5,
        out_specs=(vmem, vmem),
        scratch_shapes=[
            pltpu.VMEM((Z, CHUNKS, 2 * rows, cw), BF16),
            pltpu.VMEM((rows, cols), BF16),
            pltpu.VMEM((rows, 128), F32),
            pltpu.VMEM((2 * rows, cols), BF16),
            pltpu.VMEM((groups, CHUNKS, cw, cols), BF16),
            pltpu.VMEM((groups, CHUNKS, cw, cols), BF16),
            pltpu.VMEM((groups, CHUNKS, cw, cols), BF16),
            pltpu.VMEM((rows, modes), F32),
            pltpu.VMEM((Z, rows // Z, modes), F32),
            pltpu.VMEM((rows, modes), BF16),
            pltpu.VMEM((rows, modes), BF16),
            pltpu.VMEM((2 * rows, modes), BF16),
            pltpu.VMEM((half, modes), BF16),
            pltpu.VMEM((groups, half, modes), BF16),
            pltpu.VMEM((half, modes), BF16),
            pltpu.VMEM((C, modes // C, conds), BF16),
            pltpu.VMEM((C, modes // C, conds), BF16),
            pltpu.VMEM((C, modes // C, conds), BF16),
            dma((CHUNKS,)), dma((CHUNKS,)), dma((CHUNKS,)),
            dma((3,)), dma((3,)),
            dma((2, Z, CHUNKS)), dma((Z, CHUNKS)),
            dma((groups, CHUNKS)), dma((groups, CHUNKS)),
            dma((groups, CHUNKS)), dma((groups, CHUNKS)),
            dma((Z,)), dma((Z,)), dma((Z,)), dma((Z,)),
            dma((1,)), dma((groups,)),
            dma((2,)), dma((1,)),
            dma((C,)), dma((C,)), dma((C,)), dma((C,)),
        ],
        compiler_params=pltpu.CompilerParams(
            collective_id=0, has_side_effects=True, vmem_limit_bytes=52 * 1024 * 1024
        ),
    )(snapshots, volb, mode_vectors, mode_scale[None, :], interp_weights)


def shards(snapshots, cell_volume, mode_vectors, mode_scale, interp_weights):
    C, Z = lax.axis_size("cell"), lax.axis_size("narrow")
    rows, cols = snapshots.shape
    modes = mode_vectors.shape[1]
    fits = (
        C == 2 * Z == 8
        and cols % (2 * 128 * CHUNKS) == 0
        and rows % (16 * Z) == 0
        and modes % (16 * C) == 0
        and interp_weights.shape[0] == rows == cols // 2
        and rows * cols <= 512 * 1024
        and interp_weights.shape[1] <= 1024
        and modes <= 512
    )
    run = shards_kernel if fits else shards_xla
    return run(snapshots, cell_volume, mode_vectors, mode_scale, interp_weights)


def solution(mesh):
    return jax.shard_map(
        shards,
        mesh=mesh,
        in_specs=(P("cell", "narrow"), P("cell"), P("narrow", None), P(), P("cell", "narrow")),
        out_specs=(P("cell", "narrow"), P("cell", "narrow")),
        check_vma=False,
    )
```

```python
import functools

import jax
import jax.numpy as jnp
from jax import lax
from jax.experimental import pallas as pl
from jax.experimental.pallas import tpu as pltpu
from jax.sharding import PartitionSpec as P

F32, BF16 = jnp.float32, jnp.bfloat16
MESH = pl.DeviceIdType.MESH
CHUNKS = 4
LAG = 2


def shards_xla(snapshots, cell_volume, mode_vectors, mode_scale, interp_weights):
    f32, bf16 = jnp.float32, jnp.bfloat16
    n_cell, n_narrow = lax.axis_size("cell"), lax.axis_size("narrow")
    total_cells = snapshots.shape[0] * n_cell
    rows = interp_weights.shape[0]
    weighted = (snapshots.astype(f32) * cell_volume[:, None]).astype(bf16)

    partial_shapes = jnp.dot(snapshots, mode_vectors, preferred_element_type=f32)
    mode_shapes = lax.psum(partial_shapes, "narrow").astype(bf16)

    gathered = lax.all_gather(snapshots, "narrow", axis=1, tiled=True)
    scaled_shapes = (
        mode_shapes.astype(f32) * (cell_volume / total_cells)[:, None] * mode_scale[None, :]
    ).astype(bf16)
    partial_coeffs = lax.dot_general(
        gathered, scaled_shapes, (((0,), (0,)), ((), ())), preferred_element_type=f32
    ).astype(bf16)
    coeffs = lax.psum_scatter(partial_coeffs, "cell", scatter_dimension=0, tiled=True)
    partial_new = lax.dot_general(
        coeffs, interp_weights, (((0,), (0,)), ((), ())), preferred_element_type=f32
    )
    new_coeffs = lax.psum(partial_new, "cell").astype(bf16)
    fields = jnp.dot(mode_shapes, new_coeffs, preferred_element_type=f32).astype(bf16)

    partial_gram = (
        lax.dot_general(gathered, weighted, (((0,), (0,)), ((), ())), preferred_element_type=f32)
        / total_cells
    ).astype(bf16)
    gram = lax.psum_scatter(partial_gram, "cell", scatter_dimension=0, tiled=True)
    return (gram.astype(f32), fields)


def kernel(
    C, Z, total, s, volb, v, scale, w, gram, fields,
    sg, sp, volp, wf, gsend, grecv, rrecv, mpart, mrecv, mg, mgp, dm, csend, crecv, cb, ksend, krecv, kg,
    loc_sem, ps_sem, pr_sem, xs_sem, xr_sem, zs_sem, zr_sem, gs_sem, gr_sem, fs_sem, fr_sem,
    ms_sem, mr_sem, as_sem, ar_sem, cs_sem, cr_sem, bs_sem, br_sem,
    ks_sem, kr_sem, ls_sem, lr_sem,
):
    c, z = lax.axis_index("cell"), lax.axis_index("narrow")
    groups = C // 2
    p, k = lax.div(c, 2), lax.rem(c, 2)
    mate = 2 * p + 1 - k
    rows, cols = s.shape
    modes = v.shape[1]
    half = cols // 2
    cw = half // CHUNKS
    mrows = rows // Z
    krows = modes // C

    def remote(src, dst, ssem, rsem, cell, narrow):
        return pltpu.make_async_remote_copy(
            src_ref=src, dst_ref=dst, send_sem=ssem, recv_sem=rsem,
            device_id={"cell": cell, "narrow": narrow}, device_id_type=MESH,
        )

    def other(me, step, n):
        return lax.rem(me + step, n)

    barrier = pltpu.get_barrier_semaphore()
    for d in range(1, C):
        pl.semaphore_signal(
            barrier, inc=1, device_id={"cell": other(c, d, C), "narrow": z}, device_id_type=MESH
        )
    for d in range(1, Z):
        pl.semaphore_signal(
            barrier, inc=1, device_id={"cell": c, "narrow": other(z, d, Z)}, device_id_type=MESH
        )
    pl.semaphore_wait(barrier, C + Z - 2)

    mine = pl.ds(pl.multiple_of(k * rows, rows), rows)
    theirs = pl.ds(pl.multiple_of((1 - k) * rows, rows), rows)

    def local_copy(h):
        lanes = pl.ds(pl.multiple_of(k * half + h * cw, cw), cw)
        return pltpu.make_async_copy(s.at[:, lanes], sg.at[z, h, mine], loc_sem.at[h])

    def mate_copy(h):
        lanes = pl.ds(pl.multiple_of((1 - k) * half + h * cw, cw), cw)
        return remote(
            s.at[:, lanes], sg.at[z, h, mine], ps_sem.at[h], pr_sem.at[h], mate, z
        )

    block_copy = remote(s, sp, xs_sem.at[0], xr_sem.at[0], mate, z)
    vol_copy = remote(volb, volp, xs_sem.at[1], xr_sem.at[1], mate, z)
    for h in range(CHUNKS):
        local_copy(h).start()
        mate_copy(h).start()
    vol_copy.start()
    block_copy.start()

    mpart[...] = jnp.dot(s[...], v[...], preferred_element_type=F32)

    def shape_rows(b):
        return pl.ds(pl.multiple_of(b * mrows, mrows), mrows)

    def shape_send(d):
        t = other(z, d, Z)
        return remote(mpart.at[shape_rows(t)], mrecv.at[z], ms_sem.at[t], mr_sem.at[z], c, t)

    for d in range(1, Z):
        shape_send(d).start()

    def chain(side, b, h):
        to = jnp.minimum(z + 1, Z - 1) if side == 0 else jnp.maximum(z - 1, 0)
        return remote(sg.at[b, h], sg.at[b, h], zs_sem.at[side, b, h], zr_sem.at[b, h], c, to)

    def own_send(h):
        local_copy(h).wait()
        mate_copy(h).wait_recv()

        @pl.when(z < Z - 1)
        def _():
            chain(0, z, h).start()

        @pl.when(z > 0)
        def _():
            chain(1, z, h).start()

    for h in range(CHUNKS // 2):
        own_send(h)

    wf[mine, :] = (s[...].astype(F32) * volb[:, :1]).astype(BF16)
    vol_copy.wait_recv()
    block_copy.wait_recv()
    wf[theirs, :] = (sp[...].astype(F32) * volp[:, :1]).astype(BF16)

    def gram_send(b, h):
        return remote(
            gsend.at[b, h], grecv.at[p, h], gs_sem.at[b, h], gr_sem.at[p, h], 2 * b + k, z
        )

    def apart(b):
        return jnp.where(p // 2 == b // 2, 0, 2) + jnp.where(p % 2 == b % 2, 0, 1)

    def flip(b, d):
        row = 1 - b // 2 if d == 2 else b // 2
        col = 1 - b % 2 if d == 1 else b % 2
        return 2 * row + col

    def relays(b, h):
        odd = h % 2 == 1
        return (odd & (apart(b) == 1)) | ((h % 2 == 0) & (apart(b) == 2))

    def passes(b, h):
        return (b != p) & ((((h % 2) == 0) & (apart(b) == 1)) | (((h % 2) == 1) & (apart(b) == 2)))

    def across_send(b, h):
        to = jnp.where(h % 2 == 1, flip(b, 1), flip(b, 2))
        return remote(
            gsend.at[b, h], rrecv.at[b, h], fs_sem.at[b, h], fr_sem.at[b, h], 2 * to + k, z
        )

    def across_wait(b, h):
        return remote(
            gsend.at[b, h], rrecv.at[b, h], fs_sem.at[b, h], fr_sem.at[b, h],
            2 * other(p, 1, groups) + k, z,
        )

    def gram_term(b, h):
        term = lax.dot_general(
            sg[b, h], wf[...], (((0,), (0,)), ((), ())), preferred_element_type=F32
        ) * (1.0 / total)

        @pl.when(b == p)
        def _():
            gram[pl.ds(pl.multiple_of(h * cw, cw), cw), :] = term

        @pl.when(b != p)
        def _():
            gsend[b, h] = term.astype(BF16)

        @pl.when(apart(b) == 3)
        def _():
            across_send(b, h).start()

        @pl.when(passes(b, h))
        def _():
            gram_send(b, h).start()

    def relay(b, h):
        @pl.when(relays(b, h))
        def _():
            across_wait(b, h).wait_recv()
            gsend[b, h] = (gsend[b, h].astype(F32) + rrecv[b, h].astype(F32)).astype(BF16)
            gram_send(b, h).start()

    def relay_event(e):
        @pl.when(e >= 0)
        def _():
            t, h = e // CHUNKS, e % CHUNKS
            for side in (0, 1):
                b = z - t if side == 0 else z + t
                there = (b >= 0) if side == 0 else (b < Z) & (t > 0)

                @pl.when(there)
                def _():
                    relay(b, h)


    acc = mpart[shape_rows(z), :]
    for d in range(1, Z):
        q = other(z, d, Z)
        remote(mpart.at[shape_rows(z)], mrecv.at[q], ms_sem.at[q], mr_sem.at[q], c, q).wait_recv()
        acc = acc + mrecv[q]
    mg[shape_rows(z), :] = acc.astype(BF16)

    def shape_share(d, b):
        t = other(z, d, Z)
        return remote(mg.at[shape_rows(b)], mg.at[shape_rows(b)], as_sem.at[t], ar_sem.at[b], c, t)

    for d in range(1, Z):
        shape_share(d, z).start()

    for h in range(CHUNKS // 2, CHUNKS):
        own_send(h)

    @pl.loop(0, CHUNKS)
    def _(h):
        gram_term(z, h)
        relay_event(h - LAG)

    def hop(t, h):
        for side in (0, 1):
            b = z - t if side == 0 else z + t
            there = b >= 0 if side == 0 else b < Z
            onward = z < Z - 1 if side == 0 else z > 0

            @pl.when(there)
            def _():
                chain(side, b, h).wait_recv()

                @pl.when(onward)
                def _():
                    chain(side, b, h).start()

                gram_term(b, h)

    def hops(t, first=0, last=CHUNKS):
        @pl.loop(first, last)
        def _(h):
            hop(t, h)
            relay_event(t * CHUNKS + h - LAG)

    for d in range(1, Z):
        shape_share(d, other(z, d, Z)).wait_recv()
        shape_send(d).wait_send()
    mate_shapes = remote(mg, mgp, xs_sem.at[2], xr_sem.at[2], mate, z)
    mate_shapes.start()
    dm[mine, :] = (mg[...].astype(F32) * volb[:, :1]).astype(BF16)
    mate_shapes.wait_recv()
    dm[theirs, :] = (mgp[...].astype(F32) * volp[:, :1]).astype(BF16)
    diagonal = p == z

    def coeff_send():
        return remote(csend, crecv.at[p], cs_sem.at[0], cr_sem.at[p], 2 * z + k, z)

    def coeff_share(d):
        t = other(z, d, Z)
        return remote(cb, cb, bs_sem.at[t], br_sem.at[0], c, t)

    @pl.loop(0, CHUNKS)
    def _(h):
        at = pl.ds(pl.multiple_of(h * cw, cw), cw)
        term = lax.dot_general(
            sg[z, h], dm[...], (((0,), (0,)), ((), ())), preferred_element_type=F32
        )

        @pl.when(diagonal)
        def _():
            mpart[at, :] = term

        @pl.when(p != z)
        def _():
            csend[at, :] = term.astype(BF16)

    @pl.when(p != z)
    def _():
        coeff_send().start()

    hops(1)

    @pl.when(diagonal)
    def _():
        total_c = mpart[...]
        for d in range(1, groups):
            q = other(p, d, groups)
            remote(
                csend, crecv.at[q], cs_sem.at[0], cr_sem.at[q], 2 * q + k, z
            ).wait_recv()
            total_c = total_c + crecv[q].astype(F32)
        cb[...] = (total_c * (scale[...] * (1.0 / total))).astype(BF16)

        for d in range(1, Z):
            coeff_share(d).start()

    hops(2)

    @pl.when(p != z)
    def _():
        coeff_share(1).wait_recv()

    def new_send(t):
        return remote(ksend.at[t], krecv.at[c], ks_sem.at[t], kr_sem.at[c], t, z)

    part = lax.dot_general(cb[...], w[...], (((0,), (0,)), ((), ())), preferred_element_type=F32)
    ksend[...] = part.reshape(C, krows, w.shape[1]).astype(BF16)
    for d in range(1, C):
        new_send(other(c, d, C)).start()

    hops(3, 0, CHUNKS // 2)

    new = ksend[c].astype(F32)
    for d in range(1, C):
        q = other(c, d, C)
        remote(ksend.at[q], krecv.at[q], ks_sem.at[q], kr_sem.at[q], q, z).wait_recv()
        new = new + krecv[q].astype(F32)
    kg[c] = new.astype(BF16)

    def new_share(t, b):
        return remote(kg.at[b], kg.at[b], ls_sem.at[t], lr_sem.at[b], t, z)

    for d in range(1, C):
        new_share(other(c, d, C), c).start()

    hops(3, CHUNKS // 2)
    for e in range(Z * CHUNKS - LAG, Z * CHUNKS):
        relay_event(jnp.int32(e))

    @pl.loop(0, CHUNKS)
    def _(h):
        at = pl.ds(pl.multiple_of(h * cw, cw), cw)
        acc = gram[at, :]
        for d in (1, 2):
            q = flip(p, d)
            remote(
                gsend.at[q, h], grecv.at[q, h], gs_sem.at[q, h], gr_sem.at[q, h], 2 * q + k, z
            ).wait_recv()
            acc = acc + grecv[q, h].astype(F32)
        gram[at, :] = acc

    for d in range(1, C):
        q = other(c, d, C)
        new_share(q, q).wait_recv()
    fields[...] = jnp.dot(
        mg[...], kg[...].reshape(modes, w.shape[1]), preferred_element_type=F32
    ).astype(BF16)

    vol_copy.wait_send()
    block_copy.wait_send()
    mate_shapes.wait_send()
    for h in range(CHUNKS):
        mate_copy(h).wait_send()
    for d in range(1, Z):
        shape_share(d, z).wait_send()
    for d in range(1, C):
        new_send(other(c, d, C)).wait_send()
        new_share(other(c, d, C), c).wait_send()

    @pl.when(p != z)
    def _():
        coeff_send().wait_send()

    @pl.when(diagonal)
    def _():
        for d in range(1, Z):
            coeff_share(d).wait_send()

    @pl.loop(0, CHUNKS)
    def _(h):
        for b in range(Z):
            @pl.when((b <= z) & (z < Z - 1))
            def _():
                chain(0, b, h).wait_send()

            @pl.when((b >= z) & (z > 0))
            def _():
                chain(1, b, h).wait_send()

        for d in (1, 2):
            gram_send(flip(p, d), h).wait_send()
        across_send(flip(flip(p, 1), 2), h).wait_send()


def shards_kernel(snapshots, cell_volume, mode_vectors, mode_scale, interp_weights):
    C, Z = lax.axis_size("cell"), lax.axis_size("narrow")
    groups = C // 2
    rows, cols = snapshots.shape
    modes = mode_vectors.shape[1]
    conds = interp_weights.shape[1]
    half = cols // 2
    cw = half // CHUNKS
    dma = pltpu.SemaphoreType.DMA
    volb = jnp.broadcast_to(cell_volume[:, None], (rows, 128))
    vmem = pl.BlockSpec(memory_space=pltpu.VMEM)
    return pl.pallas_call(
        functools.partial(kernel, C, Z, rows * C),
        out_shape=(
            jax.ShapeDtypeStruct((half, cols), F32),
            jax.ShapeDtypeStruct((rows, conds), BF16),
        ),
        in_specs=[vmem] * 5,
        out_specs=(vmem, vmem),
        scratch_shapes=[
            pltpu.VMEM((Z, CHUNKS, 2 * rows, cw), BF16),
            pltpu.VMEM((rows, cols), BF16),
            pltpu.VMEM((rows, 128), F32),
            pltpu.VMEM((2 * rows, cols), BF16),
            pltpu.VMEM((groups, CHUNKS, cw, cols), BF16),
            pltpu.VMEM((groups, CHUNKS, cw, cols), BF16),
            pltpu.VMEM((groups, CHUNKS, cw, cols), BF16),
            pltpu.VMEM((rows, modes), F32),
            pltpu.VMEM((Z, rows // Z, modes), F32),
            pltpu.VMEM((rows, modes), BF16),
            pltpu.VMEM((rows, modes), BF16),
            pltpu.VMEM((2 * rows, modes), BF16),
            pltpu.VMEM((half, modes), BF16),
            pltpu.VMEM((groups, half, modes), BF16),
            pltpu.VMEM((half, modes), BF16),
            pltpu.VMEM((C, modes // C, conds), BF16),
            pltpu.VMEM((C, modes // C, conds), BF16),
            pltpu.VMEM((C, modes // C, conds), BF16),
            dma((CHUNKS,)), dma((CHUNKS,)), dma((CHUNKS,)),
            dma((3,)), dma((3,)),
            dma((2, Z, CHUNKS)), dma((Z, CHUNKS)),
            dma((groups, CHUNKS)), dma((groups, CHUNKS)),
            dma((groups, CHUNKS)), dma((groups, CHUNKS)),
            dma((Z,)), dma((Z,)), dma((Z,)), dma((Z,)),
            dma((1,)), dma((groups,)),
            dma((Z,)), dma((1,)),
            dma((C,)), dma((C,)), dma((C,)), dma((C,)),
        ],
        compiler_params=pltpu.CompilerParams(
            collective_id=0, has_side_effects=True, vmem_limit_bytes=52 * 1024 * 1024
        ),
    )(snapshots, volb, mode_vectors, mode_scale[None, :], interp_weights)


def shards(snapshots, cell_volume, mode_vectors, mode_scale, interp_weights):
    C, Z = lax.axis_size("cell"), lax.axis_size("narrow")
    rows, cols = snapshots.shape
    modes = mode_vectors.shape[1]
    fits = (
        C == 2 * Z == 8
        and cols % (2 * 128 * CHUNKS) == 0
        and rows % (16 * Z) == 0
        and modes % (16 * C) == 0
        and interp_weights.shape[0] == rows == cols // 2
        and rows * cols <= 512 * 1024
        and interp_weights.shape[1] <= 1024
        and modes <= 512
    )
    run = shards_kernel if fits else shards_xla
    return run(snapshots, cell_volume, mode_vectors, mode_scale, interp_weights)


def solution(mesh):
    return jax.shard_map(
        shards,
        mesh=mesh,
        in_specs=(P("cell", "narrow"), P("cell"), P("narrow", None), P(), P("cell", "narrow")),
        out_specs=(P("cell", "narrow"), P("cell", "narrow")),
        check_vma=False,
    )
```
